256 devices in a mesh: segment: 4 (over x_hi, core), slab: 64 (over y, z, x_lo).
Axes of the slice: x: 4 (x_hi: 2, x_lo: 2; x = x_hi * 2 + x_lo), y: 4, z: 8, core: 2. Of those that a mesh axis runs over, the one named last changes fastest.
Arguments:
- noisy_volume: float32 [2, 128, 96, 128], P(None, 'slab'), may hold values from -6 to 6
- fresh_noise: float32 [2, 128, 96, 128], P(None, 'slab', 'segment'), may hold values from -6 to 6
- coil_maps: bfloat16 [2, 32, 128, 96, 128], P(None, None, 'slab'), may hold values from -4 to 4
- kspace: float32 [2, 3072, 128, 128], P(None, 'slab'), may hold values from -10 to 10, as said below
- sample_mask: int32 [128, 128], replicated, may hold values 0 or 1
- first_weight: bfloat16 [27, 32, 2], replicated, may hold values from -0.875 to 0.875
- middle_weight: bfloat16 [27, 32, 32], replicated, may hold values from -0.21875 to 0.21875
- last_weight: bfloat16 [27, 2, 32], replicated, may hold values from -0.21875 to 0.21875
Outputs:
- next_volume: float32 [2, 128, 96, 128], P(None, 'slab', 'segment')
The draws below stay inside these ranges and needn't reach their ends.
Inputs may be any that keep to these rules, and one draw needn't show every extreme that they name: `kspace`: measured samples.
All inputs are finite; a program needn't handle non-finite values.
Results may differ from the reference program's by a relative error of at most 0.011.
Values may be sent and summed in bfloat16 or wider, within the bound.
A program may use at most 128 MiB of HBM per device.

```python
import math
import jax
import jax.numpy as jnp
from jax import lax

CH = 32
COILS = 32
H = 96
W = 128
DEPTH = 128
ROWS = 3072


def draw_kspace(key, part):
    shape = (2, ROWS, DEPTH, W)
    ramp = 0.6 + 1.8 * jnp.arange(ROWS, dtype=jnp.float32) / ROWS
    base = jax.random.truncated_normal(key, -4.0, 4.0, shape, jnp.float32)
    return base * ramp[None, :, None, None]


def set_ends(drawn, rng, low, high):
    place = [jax.random.randint(jax.random.fold_in(rng, axis), (), 0, length) for axis, length in enumerate(drawn.shape)]
    widest = drawn.shape.index(max(drawn.shape))
    neighbour = place[:widest] + [(place[widest] + 1) % drawn.shape[widest]] + place[widest + 1:]
    return drawn.at[tuple(place)].set(low).at[tuple(neighbour)].set(high)


def shard_levels(key, extent, cuts, smallest, high):
    level, own = 1.0, jax.random.fold_in(key, 6)
    for dim, parts in cuts:
        steps = jnp.exp(jax.random.uniform(jax.random.fold_in(own, dim), (parts,), jnp.float32, smallest / len(cuts), high / len(cuts)))
        level = level * jnp.repeat(steps, extent[dim] // parts).reshape([-1 if axis == dim else 1 for axis in range(len(extent))])
    return level


def centred(own_key, dims, width, reach, pieces=(), held_as=jnp.bfloat16):
    loudness = shard_levels(own_key, dims, pieces, -0.22, 0.18) if pieces else 1.0
    entries = jax.random.normal(own_key, dims, jnp.float32) * width * loudness
    return jnp.minimum(jnp.maximum(entries, -reach), reach).astype(held_as)


def setup_inputs(seed: int = 0) -> dict:
    key_of = jax.random.split(jax.random.key(seed), 9)
    return {
        "noisy_volume": centred(key_of[0], (2, DEPTH, H, W), 1.0, 6.0, ((1, 64),), jnp.float32),
        "fresh_noise": centred(key_of[1], (2, DEPTH, H, W), 1.0, 6.0, ((1, 64), (2, 4)), jnp.float32),
        "coil_maps": centred(key_of[2], (2, COILS, DEPTH, H, W), 1.0, 4.0, ((2, 64),)),
        "kspace": draw_kspace(jax.random.fold_in(key_of[8], 71), 0),
        "sample_mask": set_ends((jax.random.randint(key_of[4], (DEPTH, W), 0, 3) < 1).astype(jnp.int32), jax.random.fold_in(key_of[4], 1), 0, 1),
        "first_weight": centred(key_of[5], (27, CH, 2), 54 ** -0.5, 0.875),
        "middle_weight": centred(key_of[6], (27, CH, CH), (27 * CH) ** -0.5, 0.21875),
        "last_weight": centred(key_of[7], (27, 2, CH), (27 * CH) ** -0.5, 0.21875),
    }


ROOT_TWO_PI = math.sqrt(2.0 / math.pi)
KEEP_DENOISED = 0.55
KEEP_NOISY = 0.8
NOISE_GAIN = 0.35
GUIDANCE = 0.3

def gelu_value(values):
    inner = ROOT_TWO_PI * (values + 0.044715 * values * values * values)
    return 0.5 * values * (1.0 + jnp.tanh(inner))

def gelu_slope(values):
    inner = ROOT_TWO_PI * (values + 0.044715 * values * values * values)
    tangent = jnp.tanh(inner)
    return 0.5 * (1.0 + tangent) + 0.5 * values * (1.0 - tangent * tangent) * ROOT_TWO_PI * (1.0 + 0.134145 * values * values)

def flipped(weights):
    return jnp.transpose(weights[::-1], (0, 2, 1))

def conv_volume(values, weights):
    kernel = weights.astype(jnp.float32).reshape(3, 3, 3, weights.shape[1], weights.shape[2])
    kernel = jnp.transpose(kernel, (3, 4, 0, 1, 2))
    output = lax.conv_general_dilated(values.astype(jnp.float32)[None], kernel, (1, 1, 1), ((1, 1), (1, 1), (1, 1)), dimension_numbers=('NCDHW', 'OIDHW', 'NCDHW'), precision=lax.Precision.HIGHEST)
    return output[0]

def reference(noisy_volume, fresh_noise, coil_maps, kspace, sample_mask, first_weight, middle_weight, last_weight):
    first_pre = conv_volume(noisy_volume.astype(jnp.bfloat16), first_weight)
    first_out = gelu_value(first_pre).astype(jnp.bfloat16)
    middle_pre = conv_volume(first_out, middle_weight)
    middle_out = (first_out.astype(jnp.float32) + gelu_value(middle_pre)).astype(jnp.bfloat16)
    denoised = noisy_volume + conv_volume(middle_out, last_weight)
    sent_image = lax.optimization_barrier(denoised.astype(jnp.bfloat16)).astype(jnp.float32)
    complex_image = sent_image[0] + 1j * sent_image[1]
    sampling_weight_mask = sample_mask.astype(jnp.float32)[:, None, :]
    measured = jnp.transpose(kspace.reshape(2, COILS, H, DEPTH, W), (0, 1, 3, 2, 4))
    maps_float = coil_maps.astype(jnp.float32)

    def one_coil(running, coil_entries):
        sensitivity_real, sensitivity_imaginary, measurement_real, measurement_imaginary = coil_entries
        sensitivity = sensitivity_real + 1j * sensitivity_imaginary
        kspace_spectrum = jnp.fft.fftn(sensitivity * complex_image, norm='ortho')
        data_residual = sampling_weight_mask * (kspace_spectrum - (measurement_real + 1j * measurement_imaginary))
        back_image = jnp.fft.ifftn(data_residual, norm='ortho')
        return (running + jnp.conj(sensitivity) * back_image, None)
    start = jnp.zeros(complex_image.shape, complex_image.dtype)
    summed, unused = lax.scan(one_coil, start, (maps_float[0], maps_float[1], measured[0], measured[1]))
    data_grad = jnp.stack([jnp.real(summed), jnp.imag(summed)])
    cotangent = data_grad.astype(jnp.bfloat16)
    grad_middle = conv_volume(cotangent, flipped(last_weight)).astype(jnp.bfloat16)
    slope_middle = (grad_middle.astype(jnp.float32) * gelu_slope(middle_pre)).astype(jnp.bfloat16)
    grad_first = (grad_middle.astype(jnp.float32) + conv_volume(slope_middle, flipped(middle_weight))).astype(jnp.bfloat16)
    slope_first = (grad_first.astype(jnp.float32) * gelu_slope(first_pre)).astype(jnp.bfloat16)
    grad_input = conv_volume(slope_first, flipped(first_weight))
    return KEEP_DENOISED * denoised + KEEP_NOISY * noisy_volume + NOISE_GAIN * fresh_noise - GUIDANCE * (data_grad + grad_input)
```

```python
import math

import jax
import jax.numpy as jnp
import numpy as np
from jax import lax
from jax.sharding import PartitionSpec as P

ROOT_TWO_PI = math.sqrt(2.0 / math.pi)
KEEP_DENOISED = 0.55
KEEP_NOISY = 0.8
NOISE_GAIN = 0.35
GUIDANCE = 0.3
BF = jnp.bfloat16
F32 = jnp.float32

NY, NZ, NH = 4, 8, 2


def gelu_value(values):
    inner = ROOT_TWO_PI * (values + 0.044715 * values * values * values)
    return 0.5 * values * (1.0 + jnp.tanh(inner))


def gelu_slope(values):
    inner = ROOT_TWO_PI * (values + 0.044715 * values * values * values)
    tangent = jnp.tanh(inner)
    return 0.5 * (1.0 + tangent) + 0.5 * values * (1.0 - tangent * tangent) * ROOT_TWO_PI * (
        1.0 + 0.134145 * values * values
    )


def flipped(weights):
    return jnp.transpose(weights[::-1], (0, 2, 1))


def conv_taps(padded, weights):
    planes = padded.shape[1] - 2
    height = padded.shape[2] - 2
    across = padded.shape[3]
    framed = jnp.pad(padded, ((0, 0), (0, 0), (0, 0), (1, 1)))
    running = jnp.zeros((weights.shape[1], planes, height, across), F32)
    for a in range(3):
        for b in range(3):
            stacked = jnp.concatenate(
                [framed[:, a : a + planes, b : b + height, e : e + across] for e in range(3)],
                axis=0,
            )
            first = a * 9 + b * 3
            grouped = jnp.concatenate([weights[first + e] for e in range(3)], axis=1)
            running = running + jnp.einsum(
                "oi,izyx->ozyx", grouped, stacked, preferred_element_type=F32
            )
    return running


def slab_rim(block, width):
    count = lax.axis_size("slab")
    parts = [block]
    for step in range(1, (width + 1) // 2 + 1):
        depth = min(2, width - 2 * (step - 1))
        up = [(i, i + step) for i in range(count - step)]
        down = [(i + step, i) for i in range(count - step)]
        low = lax.ppermute(block[:, 2 - depth :], "slab", up)
        high = lax.ppermute(block[:, :depth], "slab", down)
        parts = [low] + parts + [high]
    return jnp.concatenate(parts, axis=1)


def dft_matrices(length, inverse):
    spots = np.arange(length)
    angles = 2.0 * np.pi * np.mod(np.outer(spots, spots), length) / length
    cosine, sine = np.cos(angles) / np.sqrt(length), np.sin(angles) / np.sqrt(length)
    if inverse:
        sine = -sine
    left = np.block([[cosine, sine], [-sine, cosine]])
    return jnp.asarray(left, BF), jnp.asarray(left.T, BF)


def on_device(
    noisy_volume,
    fresh_noise,
    coil_maps,
    kspace,
    sample_mask,
    first_weight,
    middle_weight,
    last_weight,
):
    segment = lax.axis_index("segment")
    slab = lax.axis_index("slab")
    quarter = 24

    maps_quarter = lax.dynamic_slice_in_dim(coil_maps, segment * quarter, quarter, 3)
    maps_sent = maps_quarter.reshape(2, NY, NZ, 2, NY, NH, 3, 128)
    maps_sent = jnp.transpose(maps_sent, (4, 2, 5, 0, 1, 6, 3, 7)).reshape(64, 48, 128)
    maps_got = lax.all_to_all(maps_sent, "slab", 0, 0, tiled=True)
    maps_here = jnp.transpose(maps_got.reshape(64, 2, 4, 3, 2, 128), (1, 2, 3, 0, 4, 5))
    maps_here = maps_here.reshape(2, 12, 128, 128).astype(F32)

    spots = np.arange(96)
    angles = 2.0 * np.pi * np.mod(np.outer(spots, spots), 96) / 96
    cosine, sine = np.cos(angles) / np.sqrt(96), np.sin(angles) / np.sqrt(96)
    table = jnp.asarray(np.stack([np.stack([cosine, -sine]), np.stack([sine, cosine])]), BF)
    half = lax.rem(slab, 2)
    table = lax.dynamic_slice(table, (0, 0, segment * quarter, half * 48), (2, 2, quarter, 48))
    lines = jnp.einsum(
        "oiyk,ikzx->yozx", table, kspace.astype(BF), preferred_element_type=F32
    ).astype(BF)
    lines = lines.reshape(8, 6 * 128, 128)
    groups = [[y * 16 + z * 2 + h for y in range(NY) for h in range(NH)] for z in range(NZ)]
    lines = lax.all_to_all(lines, "slab", 0, 0, axis_index_groups=groups, tiled=True)
    lines = lines.reshape(4, 2, 3, 2, 128, 128).astype(F32)
    measured = lines[:, 0] + lines[:, 1]
    measured = jnp.transpose(measured, (2, 0, 1, 3, 4)).reshape(2, 12, 128, 128)

    rows = jnp.pad(noisy_volume.astype(BF), ((0, 0), (0, 0), (4, 4), (0, 0)))
    rows = lax.dynamic_slice_in_dim(rows, segment * quarter, quarter + 8, 2)
    noisy_rim = slab_rim(rows, 4)
    plane = slab * 2 - 4 + jnp.arange(10)
    row = segment * quarter - 4 + jnp.arange(32)
    inside = ((plane >= 0) & (plane < 128))[:, None] & ((row >= 0) & (row < 96))[None, :]
    inside = inside.astype(F32)[:, :, None]
    first_pre = conv_taps(noisy_rim, first_weight)
    first_out = (gelu_value(first_pre) * inside[1:-1, 1:-1]).astype(BF)
    middle_pre = conv_taps(first_out, middle_weight)
    middle_out = (
        (first_out[:, 1:-1, 1:-1].astype(F32) + gelu_value(middle_pre)) * inside[2:-2, 2:-2]
    ).astype(BF)
    noisy_quarter = lax.dynamic_slice_in_dim(noisy_volume, segment * quarter, quarter, 2)
    denoised = noisy_quarter + conv_taps(middle_out[:, 1:-1, 1:-1], last_weight)

    sent = denoised.astype(BF).reshape(2, 2, NY, NH, 3, 128)
    sent = jnp.transpose(sent, (2, 3, 0, 4, 1, 5)).reshape(NY, 1, NH, 12, 128)
    sent = jnp.broadcast_to(sent, (NY, NZ, NH, 12, 128)).reshape(64, 12, 128)
    image = lax.all_to_all(sent, "slab", 0, 0, tiled=True)
    image = jnp.transpose(image.reshape(64, 2, 3, 2, 128), (1, 2, 0, 3, 4)).reshape(2, 1, 3, 128, 128)
    image = jnp.broadcast_to(image.astype(F32), (2, 4, 3, 128, 128)).reshape(2, 12, 128, 128)

    forward_left, forward_right = dft_matrices(128, False)
    inverse_left, inverse_right = dft_matrices(128, True)
    coil_real = maps_here[0] * image[0] - maps_here[1] * image[1]
    coil_imag = maps_here[0] * image[1] + maps_here[1] * image[0]
    value = jnp.concatenate([coil_real, coil_imag], axis=1).astype(BF)
    value = jnp.einsum("ab,nbx->nax", forward_left, value, preferred_element_type=F32)
    value = jnp.concatenate([value[:, :128], value[:, 128:]], axis=2).astype(BF)
    value = jnp.einsum("nzb,ba->nza", value, forward_right, preferred_element_type=F32)
    weight = sample_mask.astype(F32)
    miss_real = weight * (value[:, :, :128] - measured[0])
    miss_imag = weight * (value[:, :, 128:] - measured[1])
    value = jnp.concatenate([miss_real, miss_imag], axis=2).astype(BF)
    value = jnp.einsum("nzb,ba->nza", value, inverse_right, preferred_element_type=F32)
    value = jnp.concatenate([value[:, :, :128], value[:, :, 128:]], axis=1).astype(BF)
    value = jnp.einsum("ab,nbx->nax", inverse_left, value, preferred_element_type=F32)
    back_real, back_imag = value[:, :128], value[:, 128:]
    part_real = maps_here[0] * back_real + maps_here[1] * back_imag
    part_imag = maps_here[0] * back_imag - maps_here[1] * back_real
    part = jnp.stack([part_real, part_imag]).reshape(2, 4, 3, 128, 128).sum(1)

    part = part.astype(BF).reshape(2, 3, 64, 2, 128)
    part = jnp.transpose(part, (2, 0, 1, 3, 4)).reshape(64, 12, 128)
    part = lax.all_to_all(part, "slab", 0, 0, tiled=True)
    part = part.reshape(NY, NZ, NH, 2, 3, 2, 128).astype(F32).sum(1)
    data_grad = jnp.transpose(part, (2, 4, 0, 1, 3, 5)).reshape(2, 2, quarter, 128)

    cotangent = data_grad.astype(BF)
    segments = lax.axis_size("segment")
    up = [(i, i + 1) for i in range(segments - 1)]
    down = [(i + 1, i) for i in range(segments - 1)]
    low = lax.ppermute(cotangent[:, :, -3:], "segment", up)
    high = lax.ppermute(cotangent[:, :, :3], "segment", down)
    cotangent = slab_rim(jnp.concatenate([low, cotangent, high], axis=2), 3)
    grad_middle = conv_taps(cotangent, flipped(last_weight)).astype(BF)
    slope_middle = (
        grad_middle.astype(F32) * gelu_slope(middle_pre) * inside[2:-2, 2:-2]
    ).astype(BF)
    grad_first = (
        grad_middle[:, 1:-1, 1:-1].astype(F32) + conv_taps(slope_middle, flipped(middle_weight))
    ).astype(BF)
    slope_first = (
        grad_first.astype(F32) * gelu_slope(first_pre[:, 2:-2, 2:-2]) * inside[3:-3, 3:-3]
    ).astype(BF)
    grad_input = conv_taps(slope_first, flipped(first_weight))
    return (
        KEEP_DENOISED * denoised
        + KEEP_NOISY * noisy_quarter
        + NOISE_GAIN * fresh_noise
        - GUIDANCE * (data_grad + grad_input)
    )


def solution(mesh):
    in_specs = (
        P(None, "slab", None, None),
        P(None, "slab", "segment", None),
        P(None, None, "slab", None, None),
        P(None, "slab", None, None),
        P(),
        P(),
        P(),
        P(),
    )
    out_specs = P(None, "slab", "segment", None)
    return jax.shard_map(
        on_device, mesh=mesh, in_specs=in_specs, out_specs=out_specs, check_vma=False
    )
```
